768 devices in a mesh: gx: 16 (over y, core), gy: 12 (over z), gz: 4 (over x).
Axes of the slice: x: 4, y: 8, z: 12, core: 2. Of those that a mesh axis runs over, the one named last changes fastest.
Arguments:
- right_side: float32 [16, 12, 4, 6, 128], P('gx', 'gy', 'gz')
- self_drag: float32 [16, 12, 4, 6, 128], P('gx', 'gy', 'gz'), may hold values from 0.5 to 2
- pair_tensors: float32 [16, 12, 4, 36, 256], P('gx', 'gy', 'gz')
- pair_first: int32 [16, 12, 4, 256], P('gx', 'gy', 'gz'), may hold values from 0 to 127
- pair_second: int32 [16, 12, 4, 256], P('gx', 'gy', 'gz'), may hold values from 0 to 3455
- pair_count: int32 [16, 12, 4], P('gx', 'gy', 'gz'), may hold values from 32 to 256, as said below
- particle_count: int32 [16, 12, 4], P('gx', 'gy', 'gz'), may hold values from 48 to 128, as said below
Outputs:
- solution: float32 [16, 12, 4, 6, 128], P('gx', 'gy', 'gz')
- residual: float32 [16, 12, 4, 6, 128], P('gx', 'gy', 'gz')
The draws below stay inside these ranges and needn't reach their ends.
Inputs may be any that keep to these rules, and one draw needn't show every extreme that they name: Slots at or after pair_count of a block are unused; some block is full with 256 live pair slots in every draw. Particle slots at or after particle_count of a block are padding; some block is full in every draw. pair_second // 128 is a neighbour offset o in 0 to 26 naming the block displaced by (o//9 - 1, (o//3) mod 3 - 1, o mod 3 - 1), periodic in every dimension.
All inputs are finite; a program needn't handle non-finite values.
Results may differ from the reference program's by a relative error of at most 0.0003.
Values sent between devices are 32-bit elements; how exact they have to be, the bound alone decides.
A program may use at most 32 MiB of HBM per device.

```python
import math
import jax
import jax.numpy as jnp

BLOCK = 128
PSLOT = 256
ITERS = 2
NBX = 16
NBY = 12
NBZ = 4


def draw_right_side(key, part):
    first_key = jax.random.fold_in(jax.random.fold_in(key, 11), 0)
    along = jnp.arange(NBX, dtype=jnp.float32).reshape(-1, 1, 1, 1, 1)
    rising = 1.0 + 2.0 * along / max(NBX - 1, 1)
    shape = (NBX, NBY, NBZ, 6, BLOCK)
    base = jnp.clip(jax.random.normal(first_key, shape, jnp.float32), -6.0, 6.0)
    values = base * rising
    return values.astype(jnp.float32)


def draw_pair_tensors(key, part):
    first_key, second_key, third_key = jax.random.split(jax.random.fold_in(key, 23), 3)
    shape = (NBX, NBY, NBZ, 6, 6, PSLOT)
    raw_values = jax.random.uniform(first_key, shape, jnp.float32, -0.28, 0.28)
    coupled = 0.5 * (raw_values + jnp.swapaxes(raw_values, 3, 4))
    identity = (jnp.arange(6)[:, None] == jnp.arange(6)[None, :]).astype(jnp.float32).reshape(1, 1, 1, 6, 6, 1)
    leading = jax.random.uniform(second_key, (NBX, NBY, NBZ, 6, 1, PSLOT), jnp.float32, 1.5, 3.0)
    strength = jnp.exp(jax.random.uniform(third_key, (NBX, NBY, NBZ, 1, 1, PSLOT), jnp.float32, -3.0, -0.7))
    tensors = strength * (identity * leading + (1.0 - identity) * coupled)
    return tensors.reshape(NBX, NBY, NBZ, 36, PSLOT).astype(jnp.float32)


def draw_pair_count(key, part):
    first_key, second_key, third_key = jax.random.split(jax.random.fold_in(key, 37), 3)
    blocks = NBX * NBY * NBZ
    base = jax.random.randint(first_key, (blocks,), PSLOT // 8, PSLOT // 2 + 1)
    dense = jax.random.randint(second_key, (blocks,), 0, 6) == 0
    chosen = jax.random.randint(third_key, (), 0, blocks)
    counts = jnp.where(dense, PSLOT, base)
    counts = jnp.where(jnp.arange(blocks) == chosen, PSLOT, counts)
    return counts.reshape(NBX, NBY, NBZ).astype(jnp.int32)


def draw_particle_count(key, part):
    first_key, second_key = jax.random.split(jax.random.fold_in(key, 41))
    blocks = NBX * NBY * NBZ
    counts = jax.random.randint(first_key, (blocks,), 48, BLOCK + 1)
    chosen = jax.random.randint(second_key, (), 0, blocks)
    counts = jnp.where(jnp.arange(blocks) == chosen, BLOCK, counts)
    return counts.reshape(NBX, NBY, NBZ).astype(jnp.int32)


def with_ends(array, rng, low, high):
    longest = array.shape.index(max(array.shape))
    spots = []
    for shift in (0, 1):
        where = [jax.random.randint(jax.random.fold_in(rng, axis), (), 0, length) for axis, length in enumerate(array.shape)]
        where[longest] = (where[longest] + shift) % array.shape[longest]
        spots.append(tuple(where))
    return array.at[spots[0]].set(low).at[spots[1]].set(high)


def shard_levels(rng, shape, cuts, smallest, top_value):
    factor_of = 1.0
    for axis_at, parts in cuts:
        heights = jax.random.uniform(jax.random.fold_in(jax.random.fold_in(rng, 6), axis_at), (parts,), jnp.float32, smallest / len(cuts), top_value / len(cuts))
        factor_of = factor_of * jnp.repeat(jnp.exp(heights), shape[axis_at] // parts).reshape((-1,) + (1,) * (len(shape) - 1 - axis_at))
    return factor_of


def setup_inputs(seed: int = 0) -> dict:
    streams_of = jax.random.split(jax.random.key(seed), 8)
    right_side = draw_right_side(jax.random.fold_in(streams_of[7], 71), 0)
    self_drag = jnp.clip(jnp.exp(math.log(2.0) - 1.3862944 * jax.random.uniform(streams_of[1], (NBX, NBY, NBZ, 6, BLOCK), jnp.float32) ** shard_levels(streams_of[1], (NBX, NBY, NBZ, 6, BLOCK), ((0, 16), (1, 12), (2, 4)), -0.2, 0.2)), 0.5, 2.0)
    pair_tensors = draw_pair_tensors(jax.random.fold_in(streams_of[7], 71), 0)
    pair_first = with_ends(jax.random.randint(streams_of[3], (NBX, NBY, NBZ, PSLOT), 0, BLOCK), jax.random.fold_in(streams_of[3], 1), 0, BLOCK - 1).astype(jnp.int32)
    pair_second = with_ends(jax.random.randint(streams_of[4], (NBX, NBY, NBZ, PSLOT), 0, 27 * BLOCK), jax.random.fold_in(streams_of[4], 1), 0, (27 * BLOCK) - 1).astype(jnp.int32)
    pair_count = draw_pair_count(jax.random.fold_in(streams_of[7], 71), 0)
    particle_count = draw_particle_count(jax.random.fold_in(streams_of[7], 71), 0)
    return {"right_side": right_side, "self_drag": self_drag, "pair_tensors": pair_tensors, "pair_first": pair_first, "pair_second": pair_second, "pair_count": pair_count, "particle_count": particle_count}


def component_index(block_id, slot_id):
    component = jnp.arange(6, dtype=jnp.int32).reshape(1, 1, 1, 6, 1)
    return (block_id[:, :, :, None, :] * 6 + component) * BLOCK + slot_id[:, :, :, None, :]


def pair_force(flattened, near_index, far_index, tensors, valid_pair):
    difference = flattened[near_index] - flattened[far_index]
    shaped = tensors.reshape(tensors.shape[:3] + (6, 6, tensors.shape[-1]))
    forces = shaped[:, :, :, :, 0, :] * difference[:, :, :, 0:1, :]
    for column in range(1, 6):
        forces = forces + shaped[:, :, :, :, column, :] * difference[:, :, :, column:column + 1, :]
    forces = forces * valid_pair
    summed = jnp.zeros(flattened.shape, flattened.dtype).at[near_index].add(forces).at[far_index].add(-forces)
    return summed


def reference(right_side, self_drag, pair_tensors, pair_first, pair_second, pair_count, particle_count):
    along_x = jnp.arange(NBX, dtype=jnp.int32).reshape(-1, 1, 1, 1)
    along_y = jnp.arange(NBY, dtype=jnp.int32).reshape(1, -1, 1, 1)
    along_z = jnp.arange(NBZ, dtype=jnp.int32).reshape(1, 1, -1, 1)
    offset = pair_second // BLOCK
    far_slot = pair_second % BLOCK
    far_x = (along_x + offset // 9 - 1) % NBX
    far_y = (along_y + (offset // 3) % 3 - 1) % NBY
    far_z = (along_z + offset % 3 - 1) % NBZ
    near_block = (along_x * NBY + along_y) * NBZ + along_z + 0 * pair_first
    far_block = (far_x * NBY + far_y) * NBZ + far_z
    near_index = component_index(near_block, pair_first)
    far_index = component_index(far_block, far_slot)
    slot_count = jnp.arange(PSLOT, dtype=jnp.int32)
    valid_pair = (slot_count[None, None, None, :] < pair_count[:, :, :, None]).astype(jnp.float32)[:, :, :, None, :]
    particle_slots = jnp.arange(BLOCK, dtype=jnp.int32)
    live_mask = (particle_slots[None, None, None, :] < particle_count[:, :, :, None]).astype(jnp.float32)[:, :, :, None, :]

    def operate(vector):
        summed = pair_force(vector.reshape(-1), near_index, far_index, pair_tensors, valid_pair).reshape(vector.shape)
        return live_mask * (self_drag * vector + summed)

    residual = live_mask * right_side
    solution = jnp.zeros_like(residual)
    direction = residual
    norm_now = jnp.sum(residual * residual)
    for iteration in range(ITERS):
        applied = operate(direction)
        step_size = norm_now / jnp.sum(direction * applied)
        solution = solution + step_size * direction
        residual = residual - step_size * applied
        if iteration + 1 < ITERS:
            norm_next = jnp.sum(residual * residual)
            direction = residual + (norm_next / norm_now) * direction
            norm_now = norm_next
    return solution, residual
```

```python
import functools

import jax
import jax.numpy as jnp
from jax import lax
from jax.experimental import pallas as pl
from jax.experimental.pallas import tpu as pltpu
from jax.sharding import PartitionSpec as P

AXES = ("gx", "gy", "gz")
LANES = 128
PAIRS = 256
OFFSETS = 27
CENTRE = 13
STEPS = [(o // 9 - 1, o // 3 % 3 - 1, o % 3 - 1) for o in range(OFFSETS)]
OTHERS = [o for o in range(OFFSETS) if o != CENTRE]


def phase_steps(sizes):
    nx, ny, nz = sizes
    return (
        [(k, 0, 0) for k in range(1, nx)],
        [(0, k, 0) for k in range(1, ny)],
        [(0, 0, k) for k in range(1, nz)],
    )


def kernel(
    sizes,
    rhs_ref,
    drag_ref,
    tensor_ref,
    first_ref,
    second_ref,
    pair_count_ref,
    particle_count_ref,
    sol_ref,
    res_ref,
    near_hot,
    far_hot,
    columns,
    vec_a,
    vec_b,
    halo_a,
    halo_b,
    masked,
    part_a,
    part_b,
    back_a,
    back_b,
    *rest,
):
    phases = phase_steps(sizes)
    count = len(phases)
    own = rest[: 2 * count]
    got = rest[2 * count : 4 * count]
    halo_send, halo_recv, back_send, back_recv = rest[4 * count : 4 * count + 4]
    sums_send, sums_recv = rest[4 * count + 4 : 4 * count + 6]
    me = tuple(lax.axis_index(axis) for axis in AXES)

    def device(step):
        return tuple(lax.rem(m + (s % n), n) for m, s, n in zip(me, step, sizes))

    def opposite(step):
        return tuple(-s for s in step)

    greeted = []
    for step in [STEPS[o] for o in OTHERS] + [s for phase in phases for s in phase]:
        wrapped = tuple(s % n for s, n in zip(step, sizes))
        if wrapped not in greeted:
            greeted.append(wrapped)
    barrier = pltpu.get_barrier_semaphore()
    for step in greeted:
        pl.semaphore_signal(
            barrier, inc=1, device_id=device(step), device_id_type=pl.DeviceIdType.MESH
        )

    def remote(src, dst, send, recv, step):
        return pltpu.make_async_remote_copy(
            src_ref=src,
            dst_ref=dst,
            send_sem=send,
            recv_sem=recv,
            device_id=device(step),
            device_id_type=pl.DeviceIdType.MESH,
        )

    def rows(o):
        return pl.ds(8 * o, 8)

    def halo_copy(turn, o):
        source, target = ((vec_a, halo_a), (vec_b, halo_b))[turn]
        return remote(
            source, target.at[rows(o)], halo_send.at[turn, o], halo_recv.at[turn, o],
            opposite(STEPS[o]),
        )

    def back_copy(turn, o):
        source, target = ((part_a, back_a), (part_b, back_b))[turn]
        return remote(
            source.at[rows(o)], target.at[rows(o)], back_send.at[turn, o], back_recv.at[turn, o],
            STEPS[o],
        )

    offsets_before = [sum(len(p) for p in phases[:i]) for i in range(count)]

    def sums_copy(turn, phase, k):
        at = offsets_before[phase] + k
        return remote(
            own[turn * count + phase],
            got[turn * count + phase].at[k],
            sums_send.at[turn, at],
            sums_recv.at[turn, at],
            phases[phase][k],
        )

    live = lax.broadcasted_iota(jnp.int32, (6, LANES), 1) < particle_count_ref[0]
    vec_a[...] = jnp.zeros_like(vec_a)
    vec_b[...] = jnp.zeros_like(vec_b)
    force = jnp.where(live, rhs_ref[...], 0.0)
    vec_a[0:6, :] = force
    halo_a[rows(CENTRE), :] = vec_a[...]
    drag = drag_ref[...]
    second = second_ref[...]
    offset = lax.shift_right_logical(second, 7)
    far_slot = lax.bitwise_and(second, 127)
    slots = lax.broadcasted_iota(jnp.int32, (LANES, PAIRS), 0)
    near_hot[...] = jnp.where(slots == first_ref[...], 1.0, 0.0).astype(jnp.bfloat16)
    far_hot[...] = jnp.where(slots == far_slot, 1.0, 0.0).astype(jnp.bfloat16)
    valid = lax.broadcasted_iota(jnp.int32, (1, PAIRS), 1) < pair_count_ref[0]
    columns[...] = jnp.zeros_like(columns)
    for r in range(6):
        for c in range(6):
            row = tensor_ref[6 * r + c : 6 * r + c + 1, :]
            columns[c, r : r + 1, :] = jnp.where(valid, row, 0.0)

    def pieces(x):
        high = x.astype(jnp.bfloat16)
        rest_1 = x - high.astype(jnp.float32)
        middle = rest_1.astype(jnp.bfloat16)
        low = (rest_1 - middle.astype(jnp.float32)).astype(jnp.bfloat16)
        return high, middle, low

    def gather(x, hot):
        dots = [jnp.dot(p, hot[...], preferred_element_type=jnp.float32) for p in pieces(x)]
        return dots[0] + dots[1] + dots[2]

    def scatter(x, hot):
        dots = [
            lax.dot_general(
                p, hot[...], (((1,), (1,)), ((), ())), preferred_element_type=jnp.float32
            )
            for p in pieces(x)
        ]
        return dots[0] + dots[1] + dots[2]

    def far_values(halo):
        wide = gather(halo[...], far_hot)
        total = jnp.zeros((8, PAIRS), jnp.float32)
        for o in range(OFFSETS):
            total = jnp.where(offset == o, wide[8 * o : 8 * o + 8, :], total)
        return total

    def pair_forces(difference):
        forces = columns[0] * difference[0:1, :]
        for c in range(1, 6):
            forces = forces + columns[c] * difference[c : c + 1, :]
        return forces

    def spread(forces, part):
        for o in range(OFFSETS):
            masked[rows(o), :] = jnp.where(offset == o, forces, 0.0)
        part[...] = scatter(masked[...], far_hot)

    def folded(near_sum, part, back):
        far_sum = part[rows(CENTRE), :]
        for o in OTHERS:
            far_sum = far_sum + back[rows(o), :]
        return (near_sum - far_sum)[0:6, :]

    lane_row = lax.broadcasted_iota(jnp.int32, (1, LANES), 1)

    def packed(values):
        total = jnp.zeros((1, LANES), jnp.float32)
        for at, value in enumerate(values):
            total = jnp.where(lane_row == at, value, total)
        return total

    def pick(row, at):
        return jnp.sum(jnp.where(lane_row == at, row, 0.0), axis=1, keepdims=True)

    def sums_start(turn, phase, value):
        own[turn * count + phase][...] = value
        for k in range(len(phases[phase])):
            sums_copy(turn, phase, k).start()

    def sums_finish(turn, phase, value):
        for k in range(len(phases[phase])):
            sums_copy(turn, phase, k).wait_recv()
        return value + jnp.sum(got[turn * count + phase][...], axis=0)

    def total_of(x):
        return jnp.sum(jnp.sum(x, axis=0, keepdims=True), axis=1, keepdims=True)

    def pair_total(x):
        return x[:, :LANES] + x[:, LANES:]

    near_a = gather(vec_a[...], near_hot)

    pl.semaphore_wait(barrier, len(greeted))

    for o in OTHERS:
        halo_copy(0, o).start()
    for o in OTHERS:
        halo_copy(0, o).wait_recv()
    diff_a = near_a - far_values(halo_a)
    forces_a = pair_forces(diff_a)
    sums_now = packed(
        [
            total_of(force * force),
            total_of(drag * force * force) + total_of(pair_total(diff_a * forces_a)),
        ]
    )
    sums_start(0, 0, sums_now)
    spread(forces_a, part_a)
    for o in OTHERS:
        back_copy(0, o).start()
    near_sum_a = scatter(forces_a, near_hot)
    for o in OTHERS:
        back_copy(0, o).wait_recv()
    image_a = jnp.where(live, drag * force + folded(near_sum_a, part_a, back_a), 0.0)
    vec_b[0:6, :] = image_a
    for o in OTHERS:
        halo_copy(1, o).start()
    halo_b[rows(CENTRE), :] = vec_b[...]
    near_b = gather(vec_b[...], near_hot)
    sums_now = sums_finish(0, 0, sums_now)
    sums_start(0, 1, sums_now)
    for o in OTHERS:
        halo_copy(1, o).wait_recv()
    diff_b = near_b - far_values(halo_b)
    sums_now = sums_finish(0, 1, sums_now)
    sums_start(0, 2, sums_now)
    sums_now = sums_finish(0, 2, sums_now)
    norm_a = pick(sums_now, 0)
    curve_a = pick(sums_now, 1)
    step_a = norm_a / curve_a

    residual = force - step_a * image_a
    diff_r = diff_a - step_a * diff_b
    forces_r = pair_forces(diff_r)
    dragged = drag * residual
    sums_now = packed(
        [
            total_of(residual * residual),
            total_of(dragged * residual) + total_of(pair_total(diff_r * forces_r)),
            total_of(residual * image_a)
            + total_of(dragged * force)
            + total_of(pair_total(diff_a * forces_r)),
        ]
    )
    sums_start(1, 0, sums_now)
    spread(forces_r, part_b)
    for o in OTHERS:
        back_copy(1, o).start()
    near_sum_r = scatter(forces_r, near_hot)
    sums_now = sums_finish(1, 0, sums_now)
    sums_start(1, 1, sums_now)
    for o in OTHERS:
        back_copy(1, o).wait_recv()
    image_r = jnp.where(live, dragged + folded(near_sum_r, part_b, back_b), 0.0)
    sums_now = sums_finish(1, 1, sums_now)
    sums_start(1, 2, sums_now)
    for turn in range(2):
        for o in OTHERS:
            halo_copy(turn, o).wait_send()
            back_copy(turn, o).wait_send()
    sums_now = sums_finish(1, 2, sums_now)
    norm_b = pick(sums_now, 0)
    ratio = norm_b / norm_a
    curve_b = pick(sums_now, 1) + ratio * (pick(sums_now, 2) + ratio * curve_a)
    step_b = norm_b / curve_b
    sol_ref[...] = step_a * force + step_b * (residual + ratio * force)
    res_ref[...] = residual - step_b * (image_r + ratio * image_a)
    for turn in range(2):
        for phase in range(count):
            for k in range(len(phases[phase])):
                sums_copy(turn, phase, k).wait_send()


def body(
    sizes,
    right_side,
    self_drag,
    pair_tensors,
    pair_first,
    pair_second,
    pair_count,
    particle_count,
):
    phases = phase_steps(sizes)
    steps = sum(len(phase) for phase in phases)
    vmem = pl.BlockSpec(memory_space=pltpu.VMEM)
    smem = pl.BlockSpec(memory_space=pltpu.SMEM)
    f32 = jnp.float32
    block = jax.ShapeDtypeStruct((6, LANES), f32)
    wide = pltpu.VMEM((8 * OFFSETS, LANES), f32)
    solution_value, residual_value = pl.pallas_call(
        functools.partial(kernel, sizes),
        out_shape=(block, block),
        in_specs=[vmem] * 5 + [smem] * 2,
        out_specs=(vmem, vmem),
        scratch_shapes=[
            pltpu.VMEM((LANES, PAIRS), jnp.bfloat16),
            pltpu.VMEM((LANES, PAIRS), jnp.bfloat16),
            pltpu.VMEM((6, 8, PAIRS), f32),
            pltpu.VMEM((8, LANES), f32),
            pltpu.VMEM((8, LANES), f32),
            wide,
            wide,
            pltpu.VMEM((8 * OFFSETS, PAIRS), f32),
            wide,
            wide,
            wide,
            wide,
        ]
        + [pltpu.VMEM((1, LANES), f32) for _ in range(2 * len(phases))]
        + [pltpu.VMEM((len(phase), 1, LANES), f32) for _ in range(2) for phase in phases]
        + [pltpu.SemaphoreType.DMA((2, OFFSETS))] * 4
        + [pltpu.SemaphoreType.DMA((2, steps))] * 2,
        compiler_params=pltpu.CompilerParams(collective_id=0, has_side_effects=True),
    )(
        right_side.reshape(6, LANES),
        self_drag.reshape(6, LANES),
        pair_tensors.reshape(36, PAIRS),
        pair_first.reshape(1, PAIRS),
        pair_second.reshape(1, PAIRS),
        pair_count.reshape(1),
        particle_count.reshape(1),
    )
    shape = right_side.shape
    return solution_value.reshape(shape), residual_value.reshape(shape)


def solution(mesh):
    sizes = tuple(mesh.shape[axis] for axis in AXES)
    return jax.shard_map(
        functools.partial(body, sizes),
        mesh=mesh,
        in_specs=(
            P("gx", "gy", "gz", None, None),
            P("gx", "gy", "gz", None, None),
            P("gx", "gy", "gz", None, None),
            P("gx", "gy", "gz", None),
            P("gx", "gy", "gz", None),
            P("gx", "gy", "gz"),
            P("gx", "gy", "gz"),
        ),
        out_specs=(P("gx", "gy", "gz", None, None), P("gx", "gy", "gz", None, None)),
        check_vma=False,
    )
```

```python
import functools

import jax
import jax.numpy as jnp
from jax import lax
from jax.experimental import pallas as pl
from jax.experimental.pallas import tpu as pltpu
from jax.sharding import PartitionSpec as P

AXES = ("gx", "gy", "gz")
LANES = 128
PAIRS = 256
OFFSETS = 27
CENTRE = 13
STEPS = [(o // 9 - 1, o // 3 % 3 - 1, o % 3 - 1) for o in range(OFFSETS)]
OTHERS = sorted(
    (o for o in range(OFFSETS) if o != CENTRE), key=lambda o: -sum(abs(s) for s in STEPS[o])
)

SLOT = [o - (o > CENTRE) if o != CENTRE else OFFSETS - 1 for o in range(OFFSETS)]


def far_first(steps, lengths):
    def hops(step):
        return sum(min(s % n, -s % n) for s, n in zip(step, lengths))

    return sorted(steps, key=hops, reverse=True)


def phase_steps(sizes):
    nx, ny, nz = sizes
    lengths = (nx // 2, 2, ny, nz)
    return (
        far_first([(0, c, k, 0) for k in range(ny) for c in range(2)], lengths)[:-1],
        far_first([(j, 0, 0, k) for k in range(nz) for j in range(nx // 2)], lengths)[:-1],
    )


def kernel(
    sizes,
    rhs_ref,
    drag_ref,
    tensor_ref,
    first_ref,
    second_ref,
    pair_count_ref,
    particle_count_ref,
    out_ref,
    near_hot,
    far_hot,
    columns,
    vec_a,
    vec_b,
    halo_a,
    halo_b,
    masked,
    part_a,
    part_b,
    back_a,
    back_b,
    rhs_v,
    drag_v,
    first_v,
    second_v,
    tensor_v,
    pair_count_s,
    particle_count_s,
    drag_rows,
    load_sem,
    *rest,
):
    phases = phase_steps(sizes)
    count = len(phases)
    own = rest[: 2 * count]
    got = rest[2 * count : 4 * count]
    halo_send, halo_recv, back_send, back_recv = rest[4 * count : 4 * count + 4]
    sums_send, sums_recv = rest[4 * count + 4 : 4 * count + 6]
    loaded = (rhs_v, drag_v, first_v, second_v, tensor_v, pair_count_s, particle_count_s)
    given = (
        rhs_ref, drag_ref, first_ref, second_ref, tensor_ref, pair_count_ref, particle_count_ref,
    )
    loads = [
        pltpu.make_async_copy(src, dst, load_sem.at[at])
        for at, (src, dst) in enumerate(zip(given, loaded))
    ]
    for load in loads:
        load.start()
    me = tuple(lax.axis_index(axis) for axis in AXES)

    known = {}

    def shifted(axis, by):
        by = by % sizes[axis]
        if by == 0:
            return me[axis]
        if (axis, by) not in known:
            known[axis, by] = lax.rem(me[axis] + by, sizes[axis])
        return known[axis, by]

    def device(step):
        if len(step) == 3:
            return tuple(shifted(axis, by) for axis, by in enumerate(step))
        row, side, y, z = step
        if ("x", row, side) not in known:
            across = shifted(0, 2 * row)
            if side:
                across = across + 1 - 2 * lax.rem(across, 2)
            known["x", row, side] = across
        return known["x", row, side], shifted(1, y), shifted(2, z)

    def opposite(step):
        return tuple(-s for s in step)

    near_steps = [tuple(s % n for s, n in zip(STEPS[o], sizes)) for o in OTHERS]
    greeted = [s for phase in phases for s in phase]
    greeted = [s for s in greeted if s[1] or (2 * s[0], s[2], s[3]) not in near_steps]
    greeted = greeted + near_steps
    barrier = pltpu.get_barrier_semaphore()
    for step in greeted:
        pl.semaphore_signal(
            barrier, inc=1, device_id=device(step), device_id_type=pl.DeviceIdType.MESH
        )

    def remote(src, dst, send, recv, step):
        return pltpu.make_async_remote_copy(
            src_ref=src,
            dst_ref=dst,
            send_sem=send,
            recv_sem=recv,
            device_id=device(step),
            device_id_type=pl.DeviceIdType.MESH,
        )

    def rows(o):
        return pl.ds(8 * SLOT[o], 8)

    def wait_all(buffer, sem):
        pltpu.make_async_copy(buffer, buffer, sem).wait()

    arriving = pl.ds(0, 8 * (OFFSETS - 1))

    def halo_copy(turn, o):
        source, target = ((vec_a, halo_a), (vec_b, halo_b))[turn]
        return remote(
            source, target.at[rows(o)], halo_send.at[turn], halo_recv.at[turn],
            opposite(STEPS[o]),
        )

    def back_copy(turn, o):
        source, target = ((part_a, back_a), (part_b, back_b))[turn]
        return remote(
            source.at[rows(o)], target.at[rows(o)], back_send.at[turn], back_recv.at[turn],
            STEPS[o],
        )

    def sums_copy(turn, phase, k):
        at = turn * count + phase
        return remote(
            own[turn * count + phase],
            got[turn * count + phase].at[k],
            sums_send.at[at],
            sums_recv.at[at],
            phases[phase][k],
        )

    loads[5].wait()
    loads[6].wait()
    live = lax.broadcasted_iota(jnp.int32, (6, LANES), 1) < particle_count_s[0, 0, 0]
    vec_a[...] = jnp.zeros_like(vec_a)
    loads[0].wait()
    for r in range(6):
        vec_a[r : r + 1, :] = jnp.where(live[0:1], rhs_v[r], 0.0)
    pl.semaphore_wait(barrier, len(greeted))
    for o in OTHERS:
        halo_copy(0, o).start()
    vec_b[...] = jnp.zeros_like(vec_b)
    columns[...] = jnp.zeros_like(columns)
    loads[1].wait()
    for r in range(6):
        drag_rows[r : r + 1, :] = drag_v[r]
    force = vec_a[0:6, :]
    halo_a[rows(CENTRE), :] = vec_a[...]
    drag = drag_rows[...]
    loads[2].wait()
    loads[3].wait()
    second = second_v[...]
    offset = lax.shift_right_logical(second, 7)
    far_slot = lax.bitwise_and(second, 127)
    slots = lax.broadcasted_iota(jnp.int32, (LANES, PAIRS), 0)
    near_hot[...] = jnp.where(slots == first_v[...], 1.0, 0.0).astype(jnp.bfloat16)
    far_hot[...] = jnp.where(slots == far_slot, 1.0, 0.0).astype(jnp.bfloat16)
    valid = lax.broadcasted_iota(jnp.int32, (1, PAIRS), 1) < pair_count_s[0, 0, 0]
    loads[4].wait()
    for r in range(6):
        for c in range(6):
            columns[c, r : r + 1, :] = jnp.where(valid, tensor_v[6 * r + c], 0.0)

    def pieces(x):
        high = x.astype(jnp.bfloat16)
        rest_1 = x - high.astype(jnp.float32)
        middle = rest_1.astype(jnp.bfloat16)
        low = (rest_1 - middle.astype(jnp.float32)).astype(jnp.bfloat16)
        return high, middle, low

    def stacked(x):
        return jnp.concatenate(pieces(x), axis=0)

    def unstacked(wide):
        height = wide.shape[0] // 3
        return wide[:height] + wide[height : 2 * height] + wide[2 * height :]

    def gather(x, hot):
        return unstacked(jnp.dot(stacked(x), hot[...], preferred_element_type=jnp.float32))

    def scatter(x, hot):
        return unstacked(
            lax.dot_general(
                stacked(x),
                hot[...],
                (((1,), (1,)), ((), ())),
                preferred_element_type=jnp.float32,
            )
        )

    def far_values(halo):
        wide = gather(halo[...], far_hot)
        total = jnp.zeros((8, PAIRS), jnp.float32)
        for o in range(OFFSETS):
            total = jnp.where(offset == o, wide[8 * SLOT[o] : 8 * SLOT[o] + 8, :], total)
        return total

    def pair_forces(difference):
        forces = columns[0] * difference[0:1, :]
        for c in range(1, 6):
            forces = forces + columns[c] * difference[c : c + 1, :]
        return forces

    def spread(forces, part):
        for o in range(OFFSETS):
            masked[rows(o), :] = jnp.where(offset == o, forces, 0.0)
        part[...] = scatter(masked[...], far_hot)

    def folded(near_sum, part, back):
        far_sum = part[rows(CENTRE), :]
        for o in OTHERS:
            far_sum = far_sum + back[rows(o), :]
        return (near_sum - far_sum)[0:6, :]

    lane_row = lax.broadcasted_iota(jnp.int32, (1, LANES), 1)

    def packed(values):
        total = jnp.zeros((1, LANES), jnp.float32)
        for at, value in enumerate(values):
            total = jnp.where(lane_row == at, value, total)
        return total

    def pick(row, at):
        return jnp.sum(jnp.where(lane_row == at, row, 0.0), axis=1, keepdims=True)

    def sums_start(turn, phase, value):
        own[turn * count + phase][...] = value
        for k in range(len(phases[phase])):
            sums_copy(turn, phase, k).start()

    def sums_finish(turn, phase, value):
        wait_all(got[turn * count + phase], sums_recv.at[turn * count + phase])
        return value + jnp.sum(got[turn * count + phase][...], axis=0)

    def total_of(x):
        return jnp.sum(jnp.sum(x, axis=0, keepdims=True), axis=1, keepdims=True)

    def pair_total(x):
        return x[:, :LANES] + x[:, LANES:]

    near_a = gather(vec_a[...], near_hot)

    wait_all(halo_a.at[arriving], halo_recv.at[0])
    diff_a = near_a - far_values(halo_a)
    forces_a = pair_forces(diff_a)
    spread(forces_a, part_a)
    for o in OTHERS:
        back_copy(0, o).start()
    sums_now = packed(
        [
            total_of(force * force),
            total_of(drag * force * force) + total_of(pair_total(diff_a * forces_a)),
        ]
    )
    sums_start(0, 0, sums_now)
    near_sum_a = scatter(forces_a, near_hot)
    wait_all(back_a.at[arriving], back_recv.at[0])
    image_a = jnp.where(live, drag * force + folded(near_sum_a, part_a, back_a), 0.0)
    vec_b[0:6, :] = image_a
    for o in OTHERS:
        halo_copy(1, o).start()
    halo_b[rows(CENTRE), :] = vec_b[...]
    sums_now = sums_finish(0, 0, sums_now)
    sums_start(0, 1, sums_now)
    near_b = gather(vec_b[...], near_hot)
    wait_all(halo_b.at[arriving], halo_recv.at[1])
    diff_b = near_b - far_values(halo_b)
    sums_now = sums_finish(0, 1, sums_now)
    norm_a = pick(sums_now, 0)
    curve_a = pick(sums_now, 1)
    step_a = norm_a / curve_a

    residual = force - step_a * image_a
    diff_r = diff_a - step_a * diff_b
    forces_r = pair_forces(diff_r)
    dragged = drag * residual
    sums_now = packed(
        [
            total_of(residual * residual),
            total_of(dragged * residual) + total_of(pair_total(diff_r * forces_r)),
            total_of(residual * image_a)
            + total_of(dragged * force)
            + total_of(pair_total(diff_a * forces_r)),
        ]
    )
    sums_start(1, 0, sums_now)
    spread(forces_r, part_b)
    for o in OTHERS:
        back_copy(1, o).start()
    near_sum_r = scatter(forces_r, near_hot)
    sums_now = sums_finish(1, 0, sums_now)
    sums_start(1, 1, sums_now)
    wait_all(back_b.at[arriving], back_recv.at[1])
    image_r = jnp.where(live, dragged + folded(near_sum_r, part_b, back_b), 0.0)
    for turn, (halo, back) in enumerate(((halo_a, back_a), (halo_b, back_b))):
        wait_all(halo.at[arriving], halo_send.at[turn])
        wait_all(back.at[arriving], back_send.at[turn])
    for at in range(2 * count - 1):
        wait_all(got[at], sums_send.at[at])
    sums_now = sums_finish(1, 1, sums_now)
    norm_b = pick(sums_now, 0)
    ratio = norm_b / norm_a
    curve_b = pick(sums_now, 1) + ratio * (pick(sums_now, 2) + ratio * curve_a)
    step_b = norm_b / curve_b
    sol = step_a * force + step_b * (residual + ratio * force)
    res = residual - step_b * (image_r + ratio * image_a)
    for r in range(6):
        out_ref[0, r] = sol[r : r + 1, :]
        out_ref[1, r] = res[r : r + 1, :]
    wait_all(got[2 * count - 1], sums_send.at[2 * count - 1])


def body(
    sizes,
    right_side,
    self_drag,
    pair_tensors,
    pair_first,
    pair_second,
    pair_count,
    particle_count,
):
    phases = phase_steps(sizes)
    vmem = pl.BlockSpec(memory_space=pltpu.VMEM)
    f32 = jnp.float32
    both = jax.ShapeDtypeStruct((2, 6, 1, LANES), f32)
    wide = pltpu.VMEM((8 * OFFSETS, LANES), f32)
    both_values = pl.pallas_call(
        functools.partial(kernel, sizes),
        out_shape=both,
        in_specs=[pl.BlockSpec(memory_space=pltpu.HBM)] * 7,
        out_specs=vmem,
        scratch_shapes=[
            pltpu.VMEM((LANES, PAIRS), jnp.bfloat16),
            pltpu.VMEM((LANES, PAIRS), jnp.bfloat16),
            pltpu.VMEM((6, 8, PAIRS), f32),
            pltpu.VMEM((8, LANES), f32),
            pltpu.VMEM((8, LANES), f32),
            wide,
            wide,
            pltpu.VMEM((8 * OFFSETS, PAIRS), f32),
            wide,
            wide,
            wide,
            wide,
            pltpu.VMEM((6, 1, LANES), f32),
            pltpu.VMEM((6, 1, LANES), f32),
            pltpu.VMEM((1, PAIRS), jnp.int32),
            pltpu.VMEM((1, PAIRS), jnp.int32),
            pltpu.VMEM((36, 1, PAIRS), f32),
            pltpu.SMEM((1, 1, 1), jnp.int32),
            pltpu.SMEM((1, 1, 1), jnp.int32),
            pltpu.VMEM((6, LANES), f32),
            pltpu.SemaphoreType.DMA((7,)),
        ]
        + [pltpu.VMEM((1, LANES), f32) for _ in range(2 * len(phases))]
        + [pltpu.VMEM((len(phase), 1, LANES), f32) for _ in range(2) for phase in phases]
        + [pltpu.SemaphoreType.DMA((2,))] * 4
        + [pltpu.SemaphoreType.DMA((2 * len(phases),))] * 2,
        compiler_params=pltpu.CompilerParams(collective_id=0, has_side_effects=True),
    )(
        right_side.reshape(6, 1, LANES),
        self_drag.reshape(6, 1, LANES),
        pair_tensors.reshape(36, 1, PAIRS),
        pair_first.reshape(1, PAIRS),
        pair_second.reshape(1, PAIRS),
        pair_count,
        particle_count,
    )
    shape = right_side.shape
    return both_values[0].reshape(shape), both_values[1].reshape(shape)


def solution(mesh):
    sizes = tuple(mesh.shape[axis] for axis in AXES)
    return jax.shard_map(
        functools.partial(body, sizes),
        mesh=mesh,
        in_specs=(
            P("gx", "gy", "gz", None, None),
            P("gx", "gy", "gz", None, None),
            P("gx", "gy", "gz", None, None),
            P("gx", "gy", "gz", None),
            P("gx", "gy", "gz", None),
            P("gx", "gy", "gz"),
            P("gx", "gy", "gz"),
        ),
        out_specs=(P("gx", "gy", "gz", None, None), P("gx", "gy", "gz", None, None)),
        check_vma=False,
    )
```

```python
import functools

import jax
import jax.numpy as jnp
from jax import lax
from jax.experimental import pallas as pl
from jax.experimental.pallas import tpu as pltpu
from jax.sharding import PartitionSpec as P

AXES = ("gx", "gy", "gz")
LANES = 128
PAIRS = 256
OFFSETS = 27
CENTRE = 13
STEPS = [(o // 9 - 1, o // 3 % 3 - 1, o % 3 - 1) for o in range(OFFSETS)]
OTHERS = sorted(
    (o for o in range(OFFSETS) if o != CENTRE), key=lambda o: -sum(abs(s) for s in STEPS[o])
)

SLOT = [o - (o > CENTRE) if o != CENTRE else OFFSETS - 1 for o in range(OFFSETS)]


def far_first(steps, lengths):
    def hops(step):
        return sum(min(s % n, -s % n) for s, n in zip(step, lengths))

    return sorted(steps, key=hops, reverse=True)


def phase_steps(sizes):
    nx, ny, nz = sizes
    lengths = (nx // 2, 2, ny, nz)
    return (
        far_first([(0, c, k, 0) for k in range(ny) for c in range(2)], lengths)[:-1],
        far_first([(j, 0, 0, k) for k in range(nz) for j in range(nx // 2)], lengths)[:-1],
    )


def kernel(
    sizes,
    rhs_ref,
    drag_ref,
    tensor_ref,
    first_ref,
    second_ref,
    pair_count_ref,
    particle_count_ref,
    out_ref,
    near_hot,
    far_hot,
    columns,
    vec_a,
    vec_b,
    halo_a,
    halo_b,
    masked,
    part_a,
    part_b,
    back_a,
    back_b,
    rhs_v,
    drag_v,
    first_v,
    second_v,
    tensor_v,
    pair_count_s,
    particle_count_s,
    drag_rows,
    load_sem,
    *rest,
):
    phases = phase_steps(sizes)
    count = len(phases)
    own = rest[: 2 * count]
    got = rest[2 * count : 4 * count]
    halo_send, halo_recv, back_send, back_recv = rest[4 * count : 4 * count + 4]
    sums_send, sums_recv = rest[4 * count + 4 : 4 * count + 6]
    loaded = (rhs_v, drag_v, first_v, second_v, tensor_v, pair_count_s, particle_count_s)
    given = (
        rhs_ref, drag_ref, first_ref, second_ref, tensor_ref, pair_count_ref, particle_count_ref,
    )
    loads = [
        pltpu.make_async_copy(src, dst, load_sem.at[at])
        for at, (src, dst) in enumerate(zip(given, loaded))
    ]
    for load in loads:
        load.start()
    me = tuple(lax.axis_index(axis) for axis in AXES)

    known = {}

    def shifted(axis, by):
        by = by % sizes[axis]
        if by == 0:
            return me[axis]
        if (axis, by) not in known:
            known[axis, by] = lax.rem(me[axis] + by, sizes[axis])
        return known[axis, by]

    def device(step):
        if len(step) == 3:
            return tuple(shifted(axis, by) for axis, by in enumerate(step))
        row, side, y, z = step
        if ("x", row, side) not in known:
            across = shifted(0, 2 * row)
            if side:
                across = across + 1 - 2 * lax.rem(across, 2)
            known["x", row, side] = across
        return known["x", row, side], shifted(1, y), shifted(2, z)

    def opposite(step):
        return tuple(-s for s in step)

    near_steps = [tuple(s % n for s, n in zip(STEPS[o], sizes)) for o in OTHERS]
    greeted = [s for phase in phases for s in phase]
    greeted = [s for s in greeted if s[1] or (2 * s[0], s[2], s[3]) not in near_steps]
    greeted = near_steps + greeted
    barrier = pltpu.get_barrier_semaphore()
    for step in greeted:
        pl.semaphore_signal(
            barrier, inc=1, device_id=device(step), device_id_type=pl.DeviceIdType.MESH
        )

    def remote(src, dst, send, recv, step):
        return pltpu.make_async_remote_copy(
            src_ref=src,
            dst_ref=dst,
            send_sem=send,
            recv_sem=recv,
            device_id=device(step),
            device_id_type=pl.DeviceIdType.MESH,
        )

    def rows(o):
        return pl.ds(8 * SLOT[o], 8)

    def wait_all(buffer, sem):
        pltpu.make_async_copy(buffer, buffer, sem).wait()

    arriving = pl.ds(0, 8 * (OFFSETS - 1))

    def halo_copy(turn, o):
        source, target = ((vec_a, halo_a), (vec_b, halo_b))[turn]
        return remote(
            source, target.at[rows(o)], halo_send.at[turn], halo_recv.at[turn],
            opposite(STEPS[o]),
        )

    def back_copy(turn, o):
        source, target = ((part_a, back_a), (part_b, back_b))[turn]
        return remote(
            source.at[rows(o)], target.at[rows(o)], back_send.at[turn], back_recv.at[turn],
            STEPS[o],
        )

    def sums_copy(turn, phase, k):
        at = turn * count + phase
        return remote(
            own[turn * count + phase],
            got[turn * count + phase].at[k],
            sums_send.at[at],
            sums_recv.at[at],
            phases[phase][k],
        )

    loads[5].wait()
    loads[6].wait()
    live = lax.broadcasted_iota(jnp.int32, (6, LANES), 1) < particle_count_s[0, 0, 0]
    vec_a[...] = jnp.zeros_like(vec_a)
    loads[0].wait()
    for r in range(6):
        vec_a[r : r + 1, :] = jnp.where(live[0:1], rhs_v[r], 0.0)
    pl.semaphore_wait(barrier, len(greeted))
    for o in OTHERS:
        halo_copy(0, o).start()
    vec_b[...] = jnp.zeros_like(vec_b)
    columns[...] = jnp.zeros_like(columns)
    loads[1].wait()
    for r in range(6):
        drag_rows[r : r + 1, :] = drag_v[r]
    force = vec_a[0:6, :]
    halo_a[rows(CENTRE), :] = vec_a[...]
    drag = drag_rows[...]
    loads[2].wait()
    loads[3].wait()
    second = second_v[...]
    offset = lax.shift_right_logical(second, 7)
    far_slot = lax.bitwise_and(second, 127)
    slots = lax.broadcasted_iota(jnp.int32, (LANES, PAIRS), 0)
    near_hot[...] = jnp.where(slots == first_v[...], 1.0, 0.0).astype(jnp.bfloat16)
    far_hot[...] = jnp.where(slots == far_slot, 1.0, 0.0).astype(jnp.bfloat16)
    valid = lax.broadcasted_iota(jnp.int32, (1, PAIRS), 1) < pair_count_s[0, 0, 0]
    loads[4].wait()
    for r in range(6):
        for c in range(6):
            columns[c, r : r + 1, :] = jnp.where(valid, tensor_v[6 * r + c], 0.0)

    def pieces(x):
        high = x.astype(jnp.bfloat16)
        rest_1 = x - high.astype(jnp.float32)
        middle = rest_1.astype(jnp.bfloat16)
        low = (rest_1 - middle.astype(jnp.float32)).astype(jnp.bfloat16)
        return high, middle, low

    def stacked(x):
        return jnp.concatenate(pieces(x), axis=0)

    def unstacked(wide):
        height = wide.shape[0] // 3
        return wide[:height] + wide[height : 2 * height] + wide[2 * height :]

    def gather(x, hot):
        return unstacked(jnp.dot(stacked(x), hot[...], preferred_element_type=jnp.float32))

    def scatter(x, hot):
        return unstacked(
            lax.dot_general(
                stacked(x),
                hot[...],
                (((1,), (1,)), ((), ())),
                preferred_element_type=jnp.float32,
            )
        )

    def far_values(halo):
        wide = gather(halo[...], far_hot)
        total = jnp.zeros((8, PAIRS), jnp.float32)
        for o in range(OFFSETS):
            total = jnp.where(offset == o, wide[8 * SLOT[o] : 8 * SLOT[o] + 8, :], total)
        return total

    def pair_forces(difference):
        forces = columns[0] * difference[0:1, :]
        for c in range(1, 6):
            forces = forces + columns[c] * difference[c : c + 1, :]
        return forces

    def spread(forces, part):
        for o in range(OFFSETS):
            masked[rows(o), :] = jnp.where(offset == o, forces, 0.0)
        part[...] = scatter(masked[...], far_hot)

    def folded(near_sum, part, back):
        far_sum = part[rows(CENTRE), :]
        for o in OTHERS:
            far_sum = far_sum + back[rows(o), :]
        return (near_sum - far_sum)[0:6, :]

    lane_row = lax.broadcasted_iota(jnp.int32, (1, LANES), 1)

    def packed(values):
        total = jnp.zeros((1, LANES), jnp.float32)
        for at, value in enumerate(values):
            total = jnp.where(lane_row == at, value, total)
        return total

    def pick(row, at):
        return jnp.sum(jnp.where(lane_row == at, row, 0.0), axis=1, keepdims=True)

    def sums_start(turn, phase, value):
        own[turn * count + phase][...] = value
        for k in range(len(phases[phase])):
            sums_copy(turn, phase, k).start()

    def sums_finish(turn, phase, value):
        wait_all(got[turn * count + phase], sums_recv.at[turn * count + phase])
        return value + jnp.sum(got[turn * count + phase][...], axis=0)

    def total_of(x):
        return jnp.sum(jnp.sum(x, axis=0, keepdims=True), axis=1, keepdims=True)

    def pair_total(x):
        return x[:, :LANES] + x[:, LANES:]

    near_a = gather(vec_a[...], near_hot)

    wait_all(halo_a.at[arriving], halo_recv.at[0])
    diff_a = near_a - far_values(halo_a)
    forces_a = pair_forces(diff_a)
    sums_now = packed(
        [
            total_of(force * force),
            total_of(drag * force * force) + total_of(pair_total(diff_a * forces_a)),
        ]
    )
    sums_start(0, 0, sums_now)
    spread(forces_a, part_a)
    for o in OTHERS:
        back_copy(0, o).start()
    near_sum_a = scatter(forces_a, near_hot)
    wait_all(back_a.at[arriving], back_recv.at[0])
    image_a = jnp.where(live, drag * force + folded(near_sum_a, part_a, back_a), 0.0)
    vec_b[0:6, :] = image_a
    for o in OTHERS:
        halo_copy(1, o).start()
    halo_b[rows(CENTRE), :] = vec_b[...]
    sums_now = sums_finish(0, 0, sums_now)
    sums_start(0, 1, sums_now)
    near_b = gather(vec_b[...], near_hot)
    wait_all(halo_b.at[arriving], halo_recv.at[1])
    diff_b = near_b - far_values(halo_b)
    for phase in range(1, count - 1):
        sums_now = sums_finish(0, phase, sums_now)
        sums_start(0, phase + 1, sums_now)
    sums_now = sums_finish(0, count - 1, sums_now)
    norm_a = pick(sums_now, 0)
    curve_a = pick(sums_now, 1)
    step_a = norm_a / curve_a

    residual = force - step_a * image_a
    diff_r = diff_a - step_a * diff_b
    forces_r = pair_forces(diff_r)
    dragged = drag * residual
    sums_now = packed(
        [
            total_of(residual * residual),
            total_of(dragged * residual) + total_of(pair_total(diff_r * forces_r)),
            total_of(residual * image_a)
            + total_of(dragged * force)
            + total_of(pair_total(diff_a * forces_r)),
        ]
    )
    sums_start(1, 0, sums_now)
    spread(forces_r, part_b)
    for o in OTHERS:
        back_copy(1, o).start()
    near_sum_r = scatter(forces_r, near_hot)
    sums_now = sums_finish(1, 0, sums_now)
    sums_start(1, 1, sums_now)
    wait_all(back_b.at[arriving], back_recv.at[1])
    image_r = jnp.where(live, dragged + folded(near_sum_r, part_b, back_b), 0.0)
    for phase in range(1, count - 1):
        sums_now = sums_finish(1, phase, sums_now)
        sums_start(1, phase + 1, sums_now)
    for turn, (halo, back) in enumerate(((halo_a, back_a), (halo_b, back_b))):
        wait_all(halo.at[arriving], halo_send.at[turn])
        wait_all(back.at[arriving], back_send.at[turn])
    for at in range(2 * count - 1):
        wait_all(got[at], sums_send.at[at])
    sums_now = sums_finish(1, count - 1, sums_now)
    norm_b = pick(sums_now, 0)
    ratio = norm_b / norm_a
    curve_b = pick(sums_now, 1) + ratio * (pick(sums_now, 2) + ratio * curve_a)
    step_b = norm_b / curve_b
    sol = step_a * force + step_b * (residual + ratio * force)
    res = residual - step_b * (image_r + ratio * image_a)
    for r in range(6):
        out_ref[0, r] = sol[r : r + 1, :]
        out_ref[1, r] = res[r : r + 1, :]
    wait_all(got[2 * count - 1], sums_send.at[2 * count - 1])


def body(
    sizes,
    right_side,
    self_drag,
    pair_tensors,
    pair_first,
    pair_second,
    pair_count,
    particle_count,
):
    phases = phase_steps(sizes)
    vmem = pl.BlockSpec(memory_space=pltpu.VMEM)
    f32 = jnp.float32
    both = jax.ShapeDtypeStruct((2, 6, 1, LANES), f32)
    wide = pltpu.VMEM((8 * OFFSETS, LANES), f32)
    both_values = pl.pallas_call(
        functools.partial(kernel, sizes),
        out_shape=both,
        in_specs=[pl.BlockSpec(memory_space=pltpu.HBM)] * 7,
        out_specs=vmem,
        scratch_shapes=[
            pltpu.VMEM((LANES, PAIRS), jnp.bfloat16),
            pltpu.VMEM((LANES, PAIRS), jnp.bfloat16),
            pltpu.VMEM((6, 8, PAIRS), f32),
            pltpu.VMEM((8, LANES), f32),
            pltpu.VMEM((8, LANES), f32),
            wide,
            wide,
            pltpu.VMEM((8 * OFFSETS, PAIRS), f32),
            wide,
            wide,
            wide,
            wide,
            pltpu.VMEM((6, 1, LANES), f32),
            pltpu.VMEM((6, 1, LANES), f32),
            pltpu.VMEM((1, PAIRS), jnp.int32),
            pltpu.VMEM((1, PAIRS), jnp.int32),
            pltpu.VMEM((36, 1, PAIRS), f32),
            pltpu.SMEM((1, 1, 1), jnp.int32),
            pltpu.SMEM((1, 1, 1), jnp.int32),
            pltpu.VMEM((6, LANES), f32),
            pltpu.SemaphoreType.DMA((7,)),
        ]
        + [pltpu.VMEM((1, LANES), f32) for _ in range(2 * len(phases))]
        + [pltpu.VMEM((len(phase), 1, LANES), f32) for _ in range(2) for phase in phases]
        + [pltpu.SemaphoreType.DMA((2,))] * 4
        + [pltpu.SemaphoreType.DMA((2 * len(phases),))] * 2,
        compiler_params=pltpu.CompilerParams(collective_id=0, has_side_effects=True),
    )(
        right_side.reshape(6, 1, LANES),
        self_drag.reshape(6, 1, LANES),
        pair_tensors.reshape(36, 1, PAIRS),
        pair_first.reshape(1, PAIRS),
        pair_second.reshape(1, PAIRS),
        pair_count,
        particle_count,
    )
    shape = right_side.shape
    return both_values[0].reshape(shape), both_values[1].reshape(shape)


def solution(mesh):
    sizes = tuple(mesh.shape[axis] for axis in AXES)
    return jax.shard_map(
        functools.partial(body, sizes),
        mesh=mesh,
        in_specs=(
            P("gx", "gy", "gz", None, None),
            P("gx", "gy", "gz", None, None),
            P("gx", "gy", "gz", None, None),
            P("gx", "gy", "gz", None),
            P("gx", "gy", "gz", None),
            P("gx", "gy", "gz"),
            P("gx", "gy", "gz"),
        ),
        out_specs=(P("gx", "gy", "gz", None, None), P("gx", "gy", "gz", None, None)),
        check_vma=False,
    )
```

```python
import functools

import jax
import jax.numpy as jnp
from jax import lax
from jax.experimental import pallas as pl
from jax.experimental.pallas import tpu as pltpu
from jax.sharding import PartitionSpec as P

AXES = ("gx", "gy", "gz")
LANES = 128
PAIRS = 256
OFFSETS = 27
CENTRE = 13
STEPS = [(o // 9 - 1, o // 3 % 3 - 1, o % 3 - 1) for o in range(OFFSETS)]
OTHERS = sorted(
    (o for o in range(OFFSETS) if o != CENTRE), key=lambda o: -sum(abs(s) for s in STEPS[o])
)

SLOT = [o - (o > CENTRE) if o != CENTRE else OFFSETS - 1 for o in range(OFFSETS)]


def far_first(steps, lengths):
    def hops(step):
        return sum(min(s % n, -s % n) for s, n in zip(step, lengths))

    return sorted(steps, key=hops, reverse=True)


def phase_steps(sizes):
    nx, ny, nz = sizes
    lengths = (nx // 2, 2, ny, nz)
    return (
        far_first([(0, c, k, 0) for k in range(ny) for c in range(2)], lengths)[:-1],
        far_first([(j, 0, 0, k) for k in range(nz) for j in range(nx // 2)], lengths)[:-1],
    )


def kernel(
    sizes,
    rhs_ref,
    drag_ref,
    tensor_ref,
    first_ref,
    second_ref,
    pair_count_ref,
    particle_count_ref,
    out_ref,
    near_hot,
    far_hot,
    columns,
    vec_a,
    vec_b,
    halo_a,
    halo_b,
    masked,
    part_a,
    part_b,
    back_a,
    back_b,
    rhs_v,
    drag_v,
    first_v,
    second_v,
    tensor_v,
    pair_count_s,
    particle_count_s,
    drag_rows,
    load_sem,
    *rest,
):
    phases = phase_steps(sizes)
    count = len(phases)
    own = rest[: 2 * count]
    got = rest[2 * count : 4 * count]
    halo_send, halo_recv, back_send, back_recv = rest[4 * count : 4 * count + 4]
    sums_send, sums_recv = rest[4 * count + 4 : 4 * count + 6]
    loaded = (rhs_v, drag_v, first_v, second_v, tensor_v, pair_count_s, particle_count_s)
    given = (
        rhs_ref, drag_ref, first_ref, second_ref, tensor_ref, pair_count_ref, particle_count_ref,
    )
    loads = [
        pltpu.make_async_copy(src, dst, load_sem.at[at])
        for at, (src, dst) in enumerate(zip(given, loaded))
    ]
    for load in loads:
        load.start()
    me = tuple(lax.axis_index(axis) for axis in AXES)

    known = {}

    def shifted(axis, by):
        by = by % sizes[axis]
        if by == 0:
            return me[axis]
        if (axis, by) not in known:
            known[axis, by] = lax.rem(me[axis] + by, sizes[axis])
        return known[axis, by]

    def device(step):
        if len(step) == 3:
            return tuple(shifted(axis, by) for axis, by in enumerate(step))
        row, side, y, z = step
        if ("x", row, side) not in known:
            across = shifted(0, 2 * row)
            if side:
                across = across + 1 - 2 * lax.rem(across, 2)
            known["x", row, side] = across
        return known["x", row, side], shifted(1, y), shifted(2, z)

    def opposite(step):
        return tuple(-s for s in step)

    near_steps = [tuple(s % n for s, n in zip(STEPS[o], sizes)) for o in OTHERS]
    greeted = [s for phase in phases for s in phase]
    greeted = [s for s in greeted if s[1] or (2 * s[0], s[2], s[3]) not in near_steps]
    greeted = near_steps + greeted
    barrier = pltpu.get_barrier_semaphore()
    for step in greeted:
        pl.semaphore_signal(
            barrier, inc=1, device_id=device(step), device_id_type=pl.DeviceIdType.MESH
        )

    def remote(src, dst, send, recv, step):
        return pltpu.make_async_remote_copy(
            src_ref=src,
            dst_ref=dst,
            send_sem=send,
            recv_sem=recv,
            device_id=device(step),
            device_id_type=pl.DeviceIdType.MESH,
        )

    def rows(o):
        return pl.ds(8 * SLOT[o], 8)

    def six(o):
        return pl.ds(8 * SLOT[o], 6)

    def wait_all(buffer, sem):
        pltpu.make_async_copy(buffer, buffer, sem).wait()

    arriving = pl.ds(0, 6 * (OFFSETS - 1))

    def halo_copy(turn, o):
        source, target = ((vec_a, halo_a), (vec_b, halo_b))[turn]
        return remote(
            source.at[pl.ds(0, 6)], target.at[six(o)], halo_send.at[turn], halo_recv.at[turn],
            opposite(STEPS[o]),
        )

    def back_copy(turn, o):
        source, target = ((part_a, back_a), (part_b, back_b))[turn]
        return remote(
            source.at[six(o)], target.at[six(o)], back_send.at[turn], back_recv.at[turn],
            STEPS[o],
        )

    def sums_copy(turn, phase, k):
        at = turn * count + phase
        return remote(
            own[turn * count + phase],
            got[turn * count + phase].at[k],
            sums_send.at[at],
            sums_recv.at[at],
            phases[phase][k],
        )

    loads[5].wait()
    loads[6].wait()
    live = lax.broadcasted_iota(jnp.int32, (6, LANES), 1) < particle_count_s[0, 0, 0]
    vec_a[...] = jnp.zeros_like(vec_a)
    loads[0].wait()
    for r in range(6):
        vec_a[r : r + 1, :] = jnp.where(live[0:1], rhs_v[r], 0.0)
    pl.semaphore_wait(barrier, len(greeted))
    for o in OTHERS:
        halo_copy(0, o).start()
    vec_b[...] = jnp.zeros_like(vec_b)
    columns[...] = jnp.zeros_like(columns)
    loads[1].wait()
    for r in range(6):
        drag_rows[r : r + 1, :] = drag_v[r]
    force = vec_a[0:6, :]
    halo_a[rows(CENTRE), :] = vec_a[...]
    drag = drag_rows[...]
    loads[2].wait()
    loads[3].wait()
    second = second_v[...]
    offset = lax.shift_right_logical(second, 7)
    far_slot = lax.bitwise_and(second, 127)
    slots = lax.broadcasted_iota(jnp.int32, (LANES, PAIRS), 0)
    near_hot[...] = jnp.where(slots == first_v[...], 1.0, 0.0).astype(jnp.bfloat16)
    far_hot[...] = jnp.where(slots == far_slot, 1.0, 0.0).astype(jnp.bfloat16)
    valid = lax.broadcasted_iota(jnp.int32, (1, PAIRS), 1) < pair_count_s[0, 0, 0]
    loads[4].wait()
    for r in range(6):
        for c in range(6):
            columns[c, r : r + 1, :] = jnp.where(valid, tensor_v[6 * r + c], 0.0)

    def pieces(x):
        high = x.astype(jnp.bfloat16)
        rest_1 = x - high.astype(jnp.float32)
        middle = rest_1.astype(jnp.bfloat16)
        low = (rest_1 - middle.astype(jnp.float32)).astype(jnp.bfloat16)
        return high, middle, low

    def stacked(x):
        return jnp.concatenate(pieces(x), axis=0)

    def unstacked(wide):
        height = wide.shape[0] // 3
        return wide[:height] + wide[height : 2 * height] + wide[2 * height :]

    def gather(x, hot):
        return unstacked(jnp.dot(stacked(x), hot[...], preferred_element_type=jnp.float32))

    def scatter(x, hot):
        return unstacked(
            lax.dot_general(
                stacked(x),
                hot[...],
                (((1,), (1,)), ((), ())),
                preferred_element_type=jnp.float32,
            )
        )

    def far_values(halo):
        wide = gather(halo[...], far_hot)
        total = jnp.zeros((8, PAIRS), jnp.float32)
        for o in range(OFFSETS):
            total = jnp.where(offset == o, wide[8 * SLOT[o] : 8 * SLOT[o] + 8, :], total)
        return total

    def pair_forces(difference):
        forces = columns[0] * difference[0:1, :]
        for c in range(1, 6):
            forces = forces + columns[c] * difference[c : c + 1, :]
        return forces

    def spread(forces, part):
        for o in range(OFFSETS):
            masked[rows(o), :] = jnp.where(offset == o, forces, 0.0)
        part[...] = scatter(masked[...], far_hot)

    def folded(near_sum, part, back):
        far_sum = part[rows(CENTRE), :]
        for o in OTHERS:
            far_sum = far_sum + back[rows(o), :]
        return (near_sum - far_sum)[0:6, :]

    lane_row = lax.broadcasted_iota(jnp.int32, (1, LANES), 1)

    def packed(values):
        total = jnp.zeros((1, LANES), jnp.float32)
        for at, value in enumerate(values):
            total = jnp.where(lane_row == at, value, total)
        return total

    def pick(row, at):
        return jnp.sum(jnp.where(lane_row == at, row, 0.0), axis=1, keepdims=True)

    def sums_start(turn, phase, value):
        own[turn * count + phase][...] = value
        for k in range(len(phases[phase])):
            sums_copy(turn, phase, k).start()

    def sums_finish(turn, phase, value):
        wait_all(got[turn * count + phase], sums_recv.at[turn * count + phase])
        return value + jnp.sum(got[turn * count + phase][...], axis=0)

    def total_of(x):
        return jnp.sum(jnp.sum(x, axis=0, keepdims=True), axis=1, keepdims=True)

    def pair_total(x):
        return x[0:6, :LANES] + x[0:6, LANES:]

    near_a = gather(vec_a[...], near_hot)

    wait_all(halo_a.at[arriving], halo_recv.at[0])
    diff_a = near_a - far_values(halo_a)
    forces_a = pair_forces(diff_a)
    sums_now = packed(
        [
            total_of(force * force),
            total_of(drag * force * force) + total_of(pair_total(diff_a * forces_a)),
        ]
    )
    sums_start(0, 0, sums_now)
    spread(forces_a, part_a)
    for o in OTHERS:
        back_copy(0, o).start()
    near_sum_a = scatter(forces_a, near_hot)
    wait_all(back_a.at[arriving], back_recv.at[0])
    image_a = jnp.where(live, drag * force + folded(near_sum_a, part_a, back_a), 0.0)
    vec_b[0:6, :] = image_a
    for o in OTHERS:
        halo_copy(1, o).start()
    halo_b[rows(CENTRE), :] = vec_b[...]
    sums_now = sums_finish(0, 0, sums_now)
    sums_start(0, 1, sums_now)
    near_b = gather(vec_b[...], near_hot)
    wait_all(halo_b.at[arriving], halo_recv.at[1])
    diff_b = near_b - far_values(halo_b)
    for phase in range(1, count - 1):
        sums_now = sums_finish(0, phase, sums_now)
        sums_start(0, phase + 1, sums_now)
    sums_now = sums_finish(0, count - 1, sums_now)
    norm_a = pick(sums_now, 0)
    curve_a = pick(sums_now, 1)
    step_a = norm_a / curve_a

    residual = force - step_a * image_a
    diff_r = diff_a - step_a * diff_b
    forces_r = pair_forces(diff_r)
    dragged = drag * residual
    sums_now = packed(
        [
            total_of(residual * residual),
            total_of(dragged * residual) + total_of(pair_total(diff_r * forces_r)),
            total_of(residual * image_a)
            + total_of(dragged * force)
            + total_of(pair_total(diff_a * forces_r)),
        ]
    )
    sums_start(1, 0, sums_now)
    spread(forces_r, part_b)
    for o in OTHERS:
        back_copy(1, o).start()
    near_sum_r = scatter(forces_r, near_hot)
    sums_now = sums_finish(1, 0, sums_now)
    sums_start(1, 1, sums_now)
    wait_all(back_b.at[arriving], back_recv.at[1])
    image_r = jnp.where(live, dragged + folded(near_sum_r, part_b, back_b), 0.0)
    for phase in range(1, count - 1):
        sums_now = sums_finish(1, phase, sums_now)
        sums_start(1, phase + 1, sums_now)
    for turn, (halo, back) in enumerate(((halo_a, back_a), (halo_b, back_b))):
        wait_all(halo.at[arriving], halo_send.at[turn])
        wait_all(back.at[arriving], back_send.at[turn])
    for at in range(2 * count - 1):
        wait_all(got[at], sums_send.at[at])
    sums_now = sums_finish(1, count - 1, sums_now)
    norm_b = pick(sums_now, 0)
    ratio = norm_b / norm_a
    curve_b = pick(sums_now, 1) + ratio * (pick(sums_now, 2) + ratio * curve_a)
    step_b = norm_b / curve_b
    sol = step_a * force + step_b * (residual + ratio * force)
    res = residual - step_b * (image_r + ratio * image_a)
    for r in range(6):
        out_ref[0, r] = sol[r : r + 1, :]
        out_ref[1, r] = res[r : r + 1, :]
    wait_all(got[2 * count - 1], sums_send.at[2 * count - 1])


def body(
    sizes,
    right_side,
    self_drag,
    pair_tensors,
    pair_first,
    pair_second,
    pair_count,
    particle_count,
):
    phases = phase_steps(sizes)
    vmem = pl.BlockSpec(memory_space=pltpu.VMEM)
    f32 = jnp.float32
    both = jax.ShapeDtypeStruct((2, 6, 1, LANES), f32)
    wide = pltpu.VMEM((8 * OFFSETS, LANES), f32)
    both_values = pl.pallas_call(
        functools.partial(kernel, sizes),
        out_shape=both,
        in_specs=[pl.BlockSpec(memory_space=pltpu.HBM)] * 7,
        out_specs=vmem,
        scratch_shapes=[
            pltpu.VMEM((LANES, PAIRS), jnp.bfloat16),
            pltpu.VMEM((LANES, PAIRS), jnp.bfloat16),
            pltpu.VMEM((6, 8, PAIRS), f32),
            pltpu.VMEM((8, LANES), f32),
            pltpu.VMEM((8, LANES), f32),
            wide,
            wide,
            pltpu.VMEM((8 * OFFSETS, PAIRS), f32),
            wide,
            wide,
            wide,
            wide,
            pltpu.VMEM((6, 1, LANES), f32),
            pltpu.VMEM((6, 1, LANES), f32),
            pltpu.VMEM((1, PAIRS), jnp.int32),
            pltpu.VMEM((1, PAIRS), jnp.int32),
            pltpu.VMEM((36, 1, PAIRS), f32),
            pltpu.SMEM((1, 1, 1), jnp.int32),
            pltpu.SMEM((1, 1, 1), jnp.int32),
            pltpu.VMEM((6, LANES), f32),
            pltpu.SemaphoreType.DMA((7,)),
        ]
        + [pltpu.VMEM((1, LANES), f32) for _ in range(2 * len(phases))]
        + [pltpu.VMEM((len(phase), 1, LANES), f32) for _ in range(2) for phase in phases]
        + [pltpu.SemaphoreType.DMA((2,))] * 4
        + [pltpu.SemaphoreType.DMA((2 * len(phases),))] * 2,
        compiler_params=pltpu.CompilerParams(collective_id=0, has_side_effects=True),
    )(
        right_side.reshape(6, 1, LANES),
        self_drag.reshape(6, 1, LANES),
        pair_tensors.reshape(36, 1, PAIRS),
        pair_first.reshape(1, PAIRS),
        pair_second.reshape(1, PAIRS),
        pair_count,
        particle_count,
    )
    shape = right_side.shape
    return both_values[0].reshape(shape), both_values[1].reshape(shape)


def solution(mesh):
    sizes = tuple(mesh.shape[axis] for axis in AXES)
    return jax.shard_map(
        functools.partial(body, sizes),
        mesh=mesh,
        in_specs=(
            P("gx", "gy", "gz", None, None),
            P("gx", "gy", "gz", None, None),
            P("gx", "gy", "gz", None, None),
            P("gx", "gy", "gz", None),
            P("gx", "gy", "gz", None),
            P("gx", "gy", "gz"),
            P("gx", "gy", "gz"),
        ),
        out_specs=(P("gx", "gy", "gz", None, None), P("gx", "gy", "gz", None, None)),
        check_vma=False,
    )
```
